512 devices in a mesh: seq: 128 (over z, y, core), dp: 4 (over x).
Axes of the slice: x: 4, y: 8, z: 8, core: 2. Of those that a mesh axis runs over, the one named last changes fastest.
Arguments:
- queries: bfloat16 [65536, 20, 128], P(('dp', 'seq')), parts along dimension 0, may hold values from -6 to 6
- keys: bfloat16 [65536, 20, 128], P(('dp', 'seq')), parts along dimension 0, may hold values from -4 to 4
- values: bfloat16 [65536, 20, 128], P(('dp', 'seq')), parts along dimension 0, may hold values from -6 to 6
- out_grad: bfloat16 [65536, 20, 128], P(('dp', 'seq')), parts along dimension 0, may hold values from -96 to 96
- block_mask: int32 [20, 128, 5], replicated, may hold values from 0 to 1, as said below
Outputs:
- query_grad: bfloat16 [65536, 20, 128], P(('dp', 'seq')), parts along dimension 0
- key_grad: bfloat16 [65536, 20, 128], P(('dp', 'seq')), parts along dimension 0
- value_grad: bfloat16 [65536, 20, 128], P(('dp', 'seq')), parts along dimension 0
The draws below stay inside these ranges and needn't reach their ends.
There are 4 independent parts, one for each index of `dp`. The reference program is written for one: setup_inputs(seed, part) draws one part's arguments, and reference() takes and returns one part's arrays. A program takes and returns all parts, laid end to end along the dimension named above; an argument that names none is the same for every part. Nothing has to cross between parts.
Inputs may be any that keep to these rules, and one draw needn't show every extreme that they name: `block_mask`: entry j of row i names key block i + j - 2. The entry for j = 2 is always 1; entries naming blocks outside 0 to 127 are 0.
All inputs are finite; a program needn't handle non-finite values.
Results may differ from the reference program's by a relative error of at most 0.0075.
Values may be sent and summed in bfloat16 or wider, within the bound.
A program may use at most 64 MiB of HBM per device.

```python
import math
import jax
import jax.numpy as jnp
from jax import lax

H = 20
E = 128
BLOCK = 128
RANGE = 2
BLOCKS = 128
TOKENS = 16384


def draw_queries(key, part):
    base_key = jax.random.fold_in(key, 1)
    return jax.random.truncated_normal(base_key, -4.0, 4.0, (TOKENS, H, E), jnp.float32).astype(jnp.bfloat16)


def draw_keys(key, part):
    base_key = jax.random.fold_in(key, 2)
    return jax.random.truncated_normal(base_key, -4.0, 4.0, (TOKENS, H, E), jnp.float32).astype(jnp.bfloat16)


def draw_block_mask(key, part):
    rate_key, bit_key = jax.random.split(jax.random.fold_in(key, 5))
    breadth = 2 * RANGE + 1
    keep_rates = jax.random.randint(rate_key, (H, BLOCKS // RANGE, 1, 1), 0, 1000)
    draw_bits = jax.random.randint(bit_key, (H, BLOCKS // RANGE, RANGE, breadth), 0, 1000)
    chosen = (draw_bits < keep_rates).reshape(H, BLOCKS, breadth)
    offsets = jnp.arange(breadth) - RANGE
    target = jnp.arange(BLOCKS)[:, None] + offsets[None, :]
    inside = (target >= 0) & (target < BLOCKS)
    allowed = chosen & inside[None] | (offsets == 0)[None, None, :]
    return allowed.astype(jnp.int32)


def block_scale(own_key, dims, pieces, low, top_value):
    factor_of, own = 1.0, jax.random.fold_in(own_key, 6)
    for axis_at, blocks in pieces:
        steps = jnp.exp(jax.random.uniform(jax.random.fold_in(own, axis_at), (blocks,), jnp.float32, low / len(pieces), top_value / len(pieces)))
        factor_of = factor_of * jnp.repeat(steps, dims[axis_at] // blocks).reshape([-1 if axis == axis_at else 1 for axis in range(len(dims))])
    return factor_of


def scatter_about(rng, extent, deviation, reach, cuts=(), kind=jnp.bfloat16):
    entries = jax.random.normal(rng, extent, jnp.float32) * deviation
    if len(cuts) > 0:
        entries = block_scale(rng, extent, cuts, -0.22, 0.18) * entries
    return jnp.clip(entries, min=-reach, max=reach).astype(kind)


def setup_inputs(seed: int = 0, part: int = 0) -> dict:
    key_of = jax.random.split(jax.random.key(seed), 6)
    own_keys = jax.random.split(jax.random.fold_in(key_of[5], part), 6)
    queries = draw_queries(jax.random.fold_in(jax.random.fold_in(key_of[5], part), 71), part)
    keys = draw_keys(jax.random.fold_in(jax.random.fold_in(key_of[5], part), 71), part)
    values = scatter_about(own_keys[2], (TOKENS, H, E), 1.0, 6.0, ((0, 128),))
    out_grad = scatter_about(own_keys[3], (TOKENS, H, E), 16.0, 96.0, ((0, 128),))
    block_mask = draw_block_mask(jax.random.fold_in(key_of[5], 71), part)
    return {"queries": queries, "keys": keys, "values": values, "out_grad": out_grad, "block_mask": block_mask}


def reference(queries, keys, values, out_grad, block_mask):
    token_count, head_count, head_width = queries.shape
    block_size = BLOCK
    reach_blocks = RANGE
    padding = reach_blocks * block_size
    window = (2 * reach_blocks + 1) * block_size
    score_scale = 1.0 / math.sqrt(head_width)
    queries_wide = queries.astype(jnp.float32)
    grad_wide = out_grad.astype(jnp.float32)
    key_padded = jnp.pad(keys.astype(jnp.float32), ((padding, padding), (0, 0), (0, 0)))
    value_padded = jnp.pad(values.astype(jnp.float32), ((padding, padding), (0, 0), (0, 0)))
    block_count = token_count // block_size

    def step_block(carry, block_index):
        key_acc, value_acc = carry
        first_row = block_index * block_size
        query_rows = lax.dynamic_slice_in_dim(queries_wide, first_row, block_size, 0)
        grad_rows = lax.dynamic_slice_in_dim(grad_wide, first_row, block_size, 0)
        key_window = lax.dynamic_slice_in_dim(key_padded, first_row, window, 0)
        value_window = lax.dynamic_slice_in_dim(value_padded, first_row, window, 0)
        mask_row = lax.dynamic_index_in_dim(block_mask, block_index, 1, False)
        allowed = jnp.repeat(mask_row > 0, block_size, axis=1)
        scores = jnp.einsum('qhe,khe->hqk', query_rows, key_window) * score_scale
        scores = jnp.where(allowed[:, None, :], scores, -jnp.inf)
        row_peak = lax.optimization_barrier(jnp.max(scores, axis=2, keepdims=True))
        exponents = jnp.exp(scores - row_peak)
        weights = exponents / lax.optimization_barrier(jnp.sum(exponents, axis=2, keepdims=True))
        weights_low = lax.optimization_barrier(weights.astype(jnp.bfloat16)).astype(jnp.float32)
        output = jnp.einsum('hqk,khe->qhe', weights_low, value_window)
        row_delta = lax.optimization_barrier(jnp.sum(grad_rows * output, axis=2))
        weight_grad = jnp.einsum('qhe,khe->hqk', grad_rows, value_window)
        score_grad = weights * (weight_grad - jnp.transpose(row_delta)[:, :, None])
        score_low = lax.optimization_barrier(score_grad.astype(jnp.bfloat16)).astype(jnp.float32)
        query_grad = score_scale * jnp.einsum('hqk,khe->qhe', score_low, key_window)
        key_part = score_scale * jnp.einsum('hqk,qhe->khe', score_low, query_rows)
        value_part = jnp.einsum('hqk,qhe->khe', weights_low, grad_rows)
        key_acc = lax.dynamic_update_slice_in_dim(key_acc, lax.dynamic_slice_in_dim(key_acc, first_row, window, 0) + key_part, first_row, 0)
        value_acc = lax.dynamic_update_slice_in_dim(value_acc, lax.dynamic_slice_in_dim(value_acc, first_row, window, 0) + value_part, first_row, 0)
        return ((key_acc, value_acc), query_grad.astype(jnp.bfloat16))
    initial = (jnp.zeros(key_padded.shape, jnp.float32), jnp.zeros(value_padded.shape, jnp.float32))
    (key_acc, value_acc), query_blocks = lax.scan(step_block, initial, jnp.arange(block_count, dtype=jnp.int32))
    query_grad = query_blocks.reshape(token_count, head_count, head_width)
    key_grad = key_acc[padding:padding + token_count].astype(jnp.bfloat16)
    value_grad = value_acc[padding:padding + token_count].astype(jnp.bfloat16)
    return (query_grad, key_grad, value_grad)
```

```python
import functools
import math

import jax
import jax.numpy as jnp
from jax import lax
from jax.experimental import pallas as pl
from jax.experimental.pallas import tpu as pltpu
from jax.sharding import PartitionSpec as P

NEG = -1e30
AHEAD = 2
LAG_TOTAL = 2
LAG_GRAD = 4
LAG_OUT = 6

NT = (((1,), (1,)), ((), ()))
NN = (((1,), (0,)), ((), ()))


def dot(a, b, dims):
    return lax.dot_general(a, b, dims, preferred_element_type=jnp.float32)


def kernel(
    seq_size,
    heads,
    scale,
    q_hbm,
    k_hbm,
    v_hbm,
    g_hbm,
    mask_ref,
    dq_hbm,
    dk_hbm,
    dv_hbm,
    qg,
    kv,
    bias,
    exps,
    dps,
    w_ref,
    ds_ref,
    part,
    part_in,
    tot,
    tot_in,
    dq_own,
    dq_send,
    dq_in,
    obuf,
    recv_qg,
    recv_kv,
    recv_part,
    recv_tot,
    recv_dq,
    send_far,
    send_near,
    send_part,
    send_tot,
    send_dq,
    out_send,
    out_recv,
    out_local,
):
    nh = heads // 2
    me = lax.axis_index("seq")
    core = lax.rem(me, 2)
    other = 1 - core
    first = me - core
    left = lax.rem(first + seq_size - 2, seq_size)
    right = lax.rem(first + 2, seq_size)
    sibling = first + other
    left_mate = left + core
    right_mate = right + core
    mine = pl.ds(pl.multiple_of(core * 128, 128), 128)
    theirs = pl.ds(pl.multiple_of(other * 128, 128), 128)

    def remote(src, dst, send, recv, to):
        return pltpu.make_async_remote_copy(
            src_ref=src,
            dst_ref=dst,
            send_sem=send,
            recv_sem=recv,
            device_id={"seq": to},
            device_id_type=pl.DeviceIdType.MESH,
        )

    def wait_for(ref, sem):
        pltpu.make_async_copy(ref, ref, sem).wait()

    def span(s, c):
        return pl.ds(pl.multiple_of(s * 256 + c * 128, 128), 128)

    def load_own(h):
        src = core * nh + h
        pltpu.make_async_copy(q_hbm.at[src], qg.at[h, 0, span(1, core)], recv_qg.at[h, 1]).start()
        pltpu.make_async_copy(g_hbm.at[src], qg.at[h, 1, span(1, core)], recv_qg.at[h, 1]).start()
        pltpu.make_async_copy(k_hbm.at[src], kv.at[h, 0, mine], recv_kv.at[h]).start()
        pltpu.make_async_copy(v_hbm.at[src], kv.at[h, 1, mine], recv_kv.at[h]).start()

    def send_head(h):
        away = other * nh + h
        own_span = span(1, core)
        remote(q_hbm.at[away], qg.at[h, 0, own_span], send_near.at[0], recv_qg.at[h, 1], sibling).start()
        remote(g_hbm.at[away], qg.at[h, 1, own_span], send_near.at[1], recv_qg.at[h, 1], sibling).start()
        remote(k_hbm.at[away], kv.at[h, 0, mine], send_near.at[2], recv_kv.at[h], sibling).start()
        remote(v_hbm.at[away], kv.at[h, 1, mine], send_near.at[3], recv_kv.at[h], sibling).start()
        for half in range(2):
            src = half * nh + h
            for side, base in ((0, left), (1, right)):
                slot = 2 - 2 * side
                to = base + half
                remote(
                    q_hbm.at[src], qg.at[h, 0, span(slot, core)], send_far.at[side, 0], recv_qg.at[h, slot], to
                ).start()
                remote(
                    g_hbm.at[src], qg.at[h, 1, span(slot, core)], send_far.at[side, 1], recv_qg.at[h, slot], to
                ).start()

    for h in range(nh):
        load_own(h)

    barrier = pltpu.get_barrier_semaphore()
    for to in (left, left + 1, right, right + 1, sibling):
        pl.semaphore_signal(barrier, inc=1, device_id={"seq": to}, device_id_type=pl.DeviceIdType.MESH)
    pl.semaphore_wait(barrier, 5)

    for h in range(AHEAD):
        send_head(h)

    planes = mask_ref[...]
    block_at = lax.broadcasted_iota(jnp.int32, planes.shape, 2)
    for t in range(6):
        picked = jnp.where(block_at == first - 2 + t, planes, 0)
        allowed = jnp.max(picked, axis=2, keepdims=True)
        bias[t] = jnp.broadcast_to(jnp.where(allowed > 0, 0.0, NEG), bias.shape[1:])
    zero = jnp.zeros((128, 128), jnp.bfloat16)
    for ref in (w_ref, ds_ref):
        ref[128:256, 0:128] = zero
        ref[0:128, 640:768] = zero
    part[...] = jnp.zeros(part.shape, jnp.float32)
    tot[...] = jnp.zeros(tot.shape, jnp.float32)

    log_scale = scale * math.log2(math.e)

    def key_blocks(t):
        return (0,) if t == 0 else (1,) if t == 5 else (0, 1)

    def scores(h):
        wait_for(kv.at[h], recv_kv.at[h])
        keys = kv[h, 0]
        values = kv[h, 1]
        for s in (1, 0, 2):
            wait_for(qg.at[h, :, s * 256 : s * 256 + 256], recv_qg.at[h, s])
            raw = dot(keys, qg[h, 0, s * 256 : s * 256 + 256], NT)
            dp = dot(values, qg[h, 1, s * 256 : s * 256 + 256], NT)
            for a in range(2):
                t = 2 * s + a
                cols = slice(a * 128, a * 128 + 128)
                put = slice(t * 128, t * 128 + 128)
                logits = {}
                for b in key_blocks(t):
                    row = bias[t, b + 4 - t, pl.ds(core * nh + h, 1), :]
                    logits[b] = raw[b * 128 : b * 128 + 128, cols] * log_scale + row
                peak = functools.reduce(
                    jnp.maximum, [jnp.max(x, axis=0, keepdims=True) for x in logits.values()]
                )
                total = 0.0
                delta = 0.0
                for b, x in logits.items():
                    rows = slice(b * 128, b * 128 + 128)
                    e = jnp.exp2(x - peak)
                    g = dp[rows, cols]
                    exps[h, rows, put] = e
                    dps[h, rows, put] = g
                    total = total + jnp.sum(e, axis=0, keepdims=True)
                    delta = delta + jnp.sum(e * g, axis=0, keepdims=True)
                part[s, h, a : a + 1, :] = peak
                part[s, h, 2 + a : 3 + a, :] = total
                part[s, h, 4 + a : 5 + a, :] = delta
            if s == 0:
                remote(part.at[0, h], part_in.at[1, h], send_part.at[0], recv_part.at[1, h], left_mate).start()
            if s == 2:
                remote(part.at[2, h], part_in.at[0, h], send_part.at[1], recv_part.at[0, h], right_mate).start()

    def totals(h):
        wait_for(part_in.at[0, h], recv_part.at[0, h])
        wait_for(part_in.at[1, h], recv_part.at[1, h])
        tiles = [part[1, h], part_in[0, h], part_in[1, h]]
        peak = functools.reduce(jnp.maximum, [x[0:2] for x in tiles])
        total = 0.0
        delta = 0.0
        for x in tiles:
            f = jnp.exp2(x[0:2] - peak)
            total = total + x[2:4] * f
            delta = delta + x[4:6] * f
        inverse = 1.0 / total
        tot[h, 0:2, :] = peak
        tot[h, 2:4, :] = inverse
        tot[h, 4:6, :] = delta * inverse
        remote(tot.at[h], tot_in.at[1, h], send_tot.at[0], recv_tot.at[1, h], left_mate).start()
        remote(tot.at[h], tot_in.at[0, h], send_tot.at[1], recv_tot.at[0, h], right_mate).start()

    def give(h, which, ref):
        dst = core * nh + h
        pltpu.make_async_copy(obuf.at[which, h, mine], ref.at[dst], out_local.at[which]).start()
        remote(obuf.at[which, h, theirs], ref.at[dst], out_send.at[which], out_recv.at[which], sibling).start()

    def grads(h):
        wait_for(tot_in.at[0, h], recv_tot.at[0, h])
        wait_for(tot_in.at[1, h], recv_tot.at[1, h])
        tiles = [tot_in[0, h], tot[h], tot_in[1, h]]
        for t in range(6):
            s, a = divmod(t, 2)
            put = slice(t * 128, t * 128 + 128)
            tile = tiles[s]
            f = jnp.exp2(part[s, h, a : a + 1, :] - tile[a : a + 1]) * tile[2 + a : 3 + a]
            shift = tile[4 + a : 5 + a]
            for b in key_blocks(t):
                rows = slice(b * 128, b * 128 + 128)
                w = exps[h, rows, put] * f
                w_ref[rows, put] = w.astype(jnp.bfloat16)
                ds_ref[rows, put] = (w * (dps[h, rows, put] - shift)).astype(jnp.bfloat16)
        ds = ds_ref[...]
        dq = dot(kv[h, 0].T, ds, NN)
        dq_send[0, h] = dq[:, 0:256].astype(jnp.bfloat16)
        remote(dq_send.at[0, h], dq_in.at[1, h], send_dq.at[0], recv_dq.at[1, h], left_mate).start()
        dq_send[1, h] = dq[:, 512:768].astype(jnp.bfloat16)
        remote(dq_send.at[1, h], dq_in.at[0, h], send_dq.at[1], recv_dq.at[0, h], right_mate).start()
        dq_own[h] = dq[:, 256:512]
        obuf[1, h] = (dot(ds, qg[h, 0], NN) * scale).astype(jnp.bfloat16)
        give(h, 1, dk_hbm)
        obuf[2, h] = dot(w_ref[...], qg[h, 1], NN).astype(jnp.bfloat16)
        give(h, 2, dv_hbm)

    def outputs(h):
        wait_for(dq_in.at[0, h], recv_dq.at[0, h])
        wait_for(dq_in.at[1, h], recv_dq.at[1, h])
        dq = dq_own[h] + dq_in[0, h].astype(jnp.float32) + dq_in[1, h].astype(jnp.float32)
        obuf[0, h] = (dq * scale).T.astype(jnp.bfloat16)
        give(h, 0, dq_hbm)

    def step(i, carry):
        @pl.when(i + AHEAD < nh)
        def _():
            send_head(i + AHEAD)

        @pl.when((i >= LAG_TOTAL) & (i < nh + LAG_TOTAL))
        def _():
            totals(i - LAG_TOTAL)

        @pl.when((i >= LAG_GRAD) & (i < nh + LAG_GRAD))
        def _():
            grads(i - LAG_GRAD)

        @pl.when(i >= LAG_OUT)
        def _():
            outputs(i - LAG_OUT)

        @pl.when(i < nh)
        def _():
            scores(i)

        return carry

    lax.fori_loop(0, nh + LAG_OUT, step, 0)

    for side in range(2):
        wait_for(q_hbm, send_far.at[side, 0])
        wait_for(g_hbm, send_far.at[side, 1])
        wait_for(part.at[0], send_part.at[side])
        wait_for(tot, send_tot.at[side])
        wait_for(dq_send.at[side], send_dq.at[side])
    for which, ref in enumerate((q_hbm, g_hbm, k_hbm, v_hbm)):
        wait_for(ref.at[0:nh], send_near.at[which])
    for which, ref in enumerate((dq_hbm, dk_hbm, dv_hbm)):
        half = ref.at[0:nh]
        wait_for(half, out_local.at[which])
        wait_for(half, out_send.at[which])
        wait_for(half, out_recv.at[which])


def per_device(queries, keys, values, out_grad, block_mask, seq_size):
    tokens, heads, width = queries.shape
    nh = heads // 2
    args = [jnp.transpose(x, (1, 0, 2)) for x in (queries, keys, values, out_grad)]
    mask = jnp.transpose(block_mask, (2, 0, 1))
    out = jax.ShapeDtypeStruct((heads, tokens, width), jnp.bfloat16)
    bf16, f32 = jnp.bfloat16, jnp.float32
    dma = pltpu.SemaphoreType.DMA
    any_spec = pl.BlockSpec(memory_space=pl.ANY)
    result = pl.pallas_call(
        functools.partial(kernel, seq_size, heads, 1.0 / math.sqrt(width)),
        out_shape=(out, out, out),
        in_specs=[any_spec] * 4 + [pl.BlockSpec(memory_space=pltpu.VMEM)],
        out_specs=(any_spec,) * 3,
        scratch_shapes=[
            pltpu.VMEM((nh, 2, 768, 128), bf16),
            pltpu.VMEM((nh, 2, 256, 128), bf16),
            pltpu.VMEM((6, 5, heads, 128), f32),
            pltpu.VMEM((nh, 256, 768), f32),
            pltpu.VMEM((nh, 256, 768), f32),
            pltpu.VMEM((256, 768), bf16),
            pltpu.VMEM((256, 768), bf16),
            pltpu.VMEM((3, nh, 8, 128), f32),
            pltpu.VMEM((2, nh, 8, 128), f32),
            pltpu.VMEM((nh, 8, 128), f32),
            pltpu.VMEM((2, nh, 8, 128), f32),
            pltpu.VMEM((nh, 128, 256), f32),
            pltpu.VMEM((2, nh, 128, 256), bf16),
            pltpu.VMEM((2, nh, 128, 256), bf16),
            pltpu.VMEM((3, nh, 256, 128), bf16),
            dma((nh, 3)),
            dma((nh,)),
            dma((2, nh)),
            dma((2, nh)),
            dma((2, nh)),
            dma((2, 2)),
            dma((4,)),
            dma((2,)),
            dma((2,)),
            dma((2,)),
            dma((3,)),
            dma((3,)),
            dma((3,)),
        ],
        compiler_params=pltpu.CompilerParams(
            collective_id=0, has_side_effects=True, vmem_limit_bytes=60000 * 1024
        ),
        name="block_attention",
    )(*args, mask)
    return tuple(jnp.transpose(x, (1, 0, 2)) for x in result)


def solution(mesh):
    spec = P(("dp", "seq"), None, None)
    return jax.shard_map(
        functools.partial(per_device, seq_size=mesh.shape["seq"]),
        mesh=mesh,
        in_specs=(spec, spec, spec, spec, P()),
        out_specs=(spec, spec, spec),
        check_vma=False,
    )
```

```python
import functools
import math

import jax
import jax.numpy as jnp
from jax import lax
from jax.experimental import pallas as pl
from jax.experimental.pallas import tpu as pltpu
from jax.sharding import PartitionSpec as P

NEG = -1e30
AHEAD = 2
LAG_TOTAL = 3
LAG_GRAD = 6
LAG_OUT = 9

NT = (((1,), (1,)), ((), ()))
NN = (((1,), (0,)), ((), ()))


def dot(a, b, dims):
    return lax.dot_general(a, b, dims, preferred_element_type=jnp.float32)


def kernel(
    seq_size,
    heads,
    scale,
    q_hbm,
    k_hbm,
    v_hbm,
    g_hbm,
    mask_hbm,
    dq_out,
    dk_out,
    dv_out,
    mask_ref,
    qg,
    kv,
    bias,
    exps,
    dps,
    w_ref,
    ds_ref,
    part,
    part_in,
    tot,
    tot_in,
    dq_own,
    dq_send,
    dq_in,
    obuf,
    recv_qg,
    recv_kv,
    recv_part,
    recv_tot,
    recv_dq,
    send_far,
    send_near,
    send_part,
    send_tot,
    send_dq,
    out_send,
    out_recv,
    mask_sem,
):
    nh = heads // 2
    me = lax.axis_index("seq")
    core = lax.rem(me, 2)
    other = 1 - core
    first = me - core
    left = first - 2
    right = first + 2
    has_left = first > 0
    has_right = right < seq_size
    sibling = first + other
    left_mate = left + core
    right_mate = right + core
    mine = pl.ds(pl.multiple_of(core * 128, 128), 128)
    theirs = pl.ds(pl.multiple_of(other * 128, 128), 128)

    barrier = pltpu.get_barrier_semaphore()

    def greet(to):
        pl.semaphore_signal(barrier, inc=1, device_id={"seq": to}, device_id_type=pl.DeviceIdType.MESH)

    greet(sibling)
    for side, base, present in ((0, left, has_left), (1, right, has_right)):

        @pl.when(present)
        def _():
            greet(base)
            greet(base + 1)

    mask_copy = pltpu.make_async_copy(mask_hbm, mask_ref, mask_sem)
    mask_copy.start()

    def remote(src, dst, send, recv, to):
        return pltpu.make_async_remote_copy(
            src_ref=src,
            dst_ref=dst,
            send_sem=send,
            recv_sem=recv,
            device_id={"seq": to},
            device_id_type=pl.DeviceIdType.MESH,
        )

    def wait_for(ref, sem):
        pltpu.make_async_copy(ref, ref, sem).wait()

    def span(s, c):
        return pl.ds(pl.multiple_of(s * 256 + c * 128, 128), 128)

    def to_mate(s, src, dst, send, recv, h):
        side = s // 2
        mate = right_mate if side else left_mate
        remote(src, dst.at[1 - side, h], send.at[side], recv.at[1 - side, h], mate).start()

    def load_own(h):
        src = core * nh + h
        pltpu.make_async_copy(q_hbm.at[src], qg.at[h, 0, span(1, core)], recv_qg.at[h, 1]).start()
        pltpu.make_async_copy(g_hbm.at[src], qg.at[h, 1, span(1, core)], recv_qg.at[h, 1]).start()
        pltpu.make_async_copy(k_hbm.at[src], kv.at[h, 0, mine], recv_kv.at[h]).start()
        pltpu.make_async_copy(v_hbm.at[src], kv.at[h, 1, mine], recv_kv.at[h]).start()

    def send_head(h):
        away = other * nh + h
        own_span = span(1, core)
        remote(q_hbm.at[away], qg.at[h, 0, own_span], send_near.at[0], recv_qg.at[h, 1], sibling).start()
        remote(g_hbm.at[away], qg.at[h, 1, own_span], send_near.at[1], recv_qg.at[h, 1], sibling).start()
        remote(k_hbm.at[away], kv.at[h, 0, mine], send_near.at[2], recv_kv.at[h], sibling).start()
        remote(v_hbm.at[away], kv.at[h, 1, mine], send_near.at[3], recv_kv.at[h], sibling).start()
        for side, base, present in ((0, left, has_left), (1, right, has_right)):
            slot = 2 - 2 * side

            @pl.when(present)
            def _():
                for half in range(2):
                    src = half * nh + h
                    to = base + half
                    remote(
                        q_hbm.at[src], qg.at[h, 0, span(slot, core)], send_far.at[side, 0], recv_qg.at[h, slot], to
                    ).start()
                    remote(
                        g_hbm.at[src], qg.at[h, 1, span(slot, core)], send_far.at[side, 1], recv_qg.at[h, slot], to
                    ).start()

    pl.semaphore_wait(barrier, 1 + 2 * has_left.astype(jnp.int32) + 2 * has_right.astype(jnp.int32))

    for h in range(AHEAD):
        send_head(h)
    for h in range(nh):
        load_own(h)

    mask_copy.wait()
    planes = mask_ref[...]
    block_at = lax.broadcasted_iota(jnp.int32, planes.shape, 2)
    for t in range(6):
        picked = jnp.where(block_at == first - 2 + t, planes, 0)
        allowed = jnp.max(picked, axis=2, keepdims=True)
        bias[t] = jnp.broadcast_to(jnp.where(allowed > 0, 0.0, NEG), bias.shape[1:])
    for side, present in ((0, has_left), (1, has_right)):

        @pl.when(jnp.logical_not(present))
        def _():
            edge = slice(512 * side, 512 * side + 256)
            qg[:, :, edge, :] = jnp.zeros((nh, 2, 256, 128), jnp.bfloat16)
            part_in[side, :, 0:2, :] = jnp.full((nh, 2, 128), NEG, jnp.float32)
            part_in[side, :, 2:8, :] = jnp.zeros((nh, 6, 128), jnp.float32)
            tot_in[side] = jnp.zeros(tot_in.shape[1:], jnp.float32)
            dq_in[side] = jnp.zeros(dq_in.shape[1:], jnp.bfloat16)

    zero = jnp.zeros((128, 128), jnp.bfloat16)
    for ref in (w_ref, ds_ref):
        ref[128:256, 0:128] = zero
        ref[0:128, 640:768] = zero
    part[...] = jnp.zeros(part.shape, jnp.float32)
    tot[...] = jnp.zeros(tot.shape, jnp.float32)

    log_scale = scale * math.log2(math.e)

    def on_side(s, act):
        if s == 1:
            act()
        else:
            pl.when(has_left if s == 0 else has_right)(act)

    def key_blocks(t):
        return (0,) if t == 0 else (1,) if t == 5 else (0, 1)

    def scores(h):
        wait_for(kv.at[h], recv_kv.at[h])
        keys = kv[h, 0]
        values = kv[h, 1]
        for s in (1, 0, 2):
            on_side(s, lambda: wait_for(qg.at[h, :, s * 256 : s * 256 + 256], recv_qg.at[h, s]))
            raw = dot(keys, qg[h, 0, s * 256 : s * 256 + 256], NT)
            dp = dot(values, qg[h, 1, s * 256 : s * 256 + 256], NT)
            for a in range(2):
                t = 2 * s + a
                cols = slice(a * 128, a * 128 + 128)
                put = slice(t * 128, t * 128 + 128)
                logits = {}
                for b in key_blocks(t):
                    row = bias[t, b + 4 - t, pl.ds(core * nh + h, 1), :]
                    logits[b] = raw[b * 128 : b * 128 + 128, cols] * log_scale + row
                peak = functools.reduce(
                    jnp.maximum, [jnp.max(x, axis=0, keepdims=True) for x in logits.values()]
                )
                total = 0.0
                delta = 0.0
                for b, x in logits.items():
                    rows = slice(b * 128, b * 128 + 128)
                    e = jnp.exp2(x - peak)
                    g = dp[rows, cols]
                    exps[h, rows, put] = e
                    dps[h, rows, put] = g
                    total = total + jnp.sum(e, axis=0, keepdims=True)
                    delta = delta + jnp.sum(e * g, axis=0, keepdims=True)
                part[s, h, a : a + 1, :] = peak
                part[s, h, 2 + a : 3 + a, :] = total
                part[s, h, 4 + a : 5 + a, :] = delta
            if s != 1:
                on_side(s, lambda: to_mate(s, part.at[s, h], part_in, send_part, recv_part, h))

    def totals(h):
        for s in (0, 2):
            on_side(s, lambda: wait_for(part_in.at[s // 2, h], recv_part.at[s // 2, h]))
        tiles = [part[1, h], part_in[0, h], part_in[1, h]]
        peak = functools.reduce(jnp.maximum, [x[0:2] for x in tiles])
        total = 0.0
        delta = 0.0
        for x in tiles:
            f = jnp.exp2(x[0:2] - peak)
            total = total + x[2:4] * f
            delta = delta + x[4:6] * f
        inverse = 1.0 / total
        tot[h, 0:2, :] = peak
        tot[h, 2:4, :] = inverse
        tot[h, 4:6, :] = delta * inverse
        for s in (0, 2):
            on_side(s, lambda: to_mate(s, tot.at[h], tot_in, send_tot, recv_tot, h))

    def give(h, which, out, value):
        value = value.astype(jnp.bfloat16)
        obuf[which, h] = value
        out[core * nh + h] = obuf[which, h, mine]
        remote(
            obuf.at[which, h, theirs], out.at[core * nh + h], out_send.at[which], out_recv.at[which], sibling
        ).start()

    def grads(h):
        for s in (0, 2):
            on_side(s, lambda: wait_for(tot_in.at[s // 2, h], recv_tot.at[s // 2, h]))
        tiles = [tot_in[0, h], tot[h], tot_in[1, h]]
        for t in range(6):
            s, a = divmod(t, 2)
            put = slice(t * 128, t * 128 + 128)
            tile = tiles[s]
            f = jnp.exp2(part[s, h, a : a + 1, :] - tile[a : a + 1]) * tile[2 + a : 3 + a]
            shift = tile[4 + a : 5 + a]
            for b in key_blocks(t):
                rows = slice(b * 128, b * 128 + 128)
                w = exps[h, rows, put] * f
                w_ref[rows, put] = w.astype(jnp.bfloat16)
                ds_ref[rows, put] = (w * (dps[h, rows, put] - shift)).astype(jnp.bfloat16)
        ds = ds_ref[...]
        dq = dot(kv[h, 0].T, ds, NN)
        for s in (0, 2):
            dq_send[s // 2, h] = dq[:, s * 256 : s * 256 + 256].astype(jnp.bfloat16)
            on_side(s, lambda: to_mate(s, dq_send.at[s // 2, h], dq_in, send_dq, recv_dq, h))
        dq_own[h] = dq[:, 256:512]
        give(h, 1, dk_out, dot(ds, qg[h, 0], NN) * scale)
        give(h, 2, dv_out, dot(w_ref[...], qg[h, 1], NN))

    def outputs(h):
        for s in (0, 2):
            on_side(s, lambda: wait_for(dq_in.at[s // 2, h], recv_dq.at[s // 2, h]))
        dq = dq_own[h] + dq_in[0, h].astype(jnp.float32) + dq_in[1, h].astype(jnp.float32)
        give(h, 0, dq_out, (dq * scale).T)

    def step(i, carry):
        @pl.when(i + AHEAD < nh)
        def _():
            send_head(i + AHEAD)

        @pl.when((i >= LAG_TOTAL) & (i < nh + LAG_TOTAL))
        def _():
            totals(i - LAG_TOTAL)

        @pl.when((i >= LAG_GRAD) & (i < nh + LAG_GRAD))
        def _():
            grads(i - LAG_GRAD)

        @pl.when(i >= LAG_OUT)
        def _():
            outputs(i - LAG_OUT)

        @pl.when(i < nh)
        def _():
            scores(i)

        return carry

    lax.fori_loop(0, nh + LAG_OUT, step, 0)

    for side, present in ((0, has_left), (1, has_right)):

        @pl.when(present)
        def _():
            wait_for(q_hbm, send_far.at[side, 0])
            wait_for(g_hbm, send_far.at[side, 1])
            wait_for(part.at[0], send_part.at[side])
            wait_for(tot, send_tot.at[side])
            wait_for(dq_send.at[side], send_dq.at[side])

    for which, ref in enumerate((q_hbm, g_hbm, k_hbm, v_hbm)):
        wait_for(ref.at[0:nh], send_near.at[which])
    for which, ref in enumerate((dq_out, dk_out, dv_out)):
        half = ref.at[0:nh]
        wait_for(half, out_send.at[which])
        wait_for(half, out_recv.at[which])


def store(dq_ref, dk_ref, dv_ref, dq_hbm, dk_hbm, dv_hbm, sem):
    copies = [
        pltpu.make_async_copy(src, dst, sem.at[i])
        for i, (src, dst) in enumerate(((dq_ref, dq_hbm), (dk_ref, dk_hbm), (dv_ref, dv_hbm)))
    ]
    for copy in copies:
        copy.start()
    for copy in copies:
        copy.wait()


def per_device(queries, keys, values, out_grad, block_mask, seq_size):
    tokens, heads, width = queries.shape
    nh = heads // 2
    args = [jnp.transpose(x, (1, 0, 2)) for x in (queries, keys, values, out_grad)]
    mask = jnp.transpose(block_mask, (2, 0, 1))
    out = jax.ShapeDtypeStruct((heads, tokens, width), jnp.bfloat16)
    bf16, f32 = jnp.bfloat16, jnp.float32
    dma = pltpu.SemaphoreType.DMA
    hbm_spec = pl.BlockSpec(memory_space=pltpu.HBM)
    vmem_spec = pl.BlockSpec(memory_space=pltpu.VMEM)
    result = pl.pallas_call(
        functools.partial(kernel, seq_size, heads, 1.0 / math.sqrt(width)),
        out_shape=(out, out, out),
        in_specs=[hbm_spec] * 5,
        out_specs=(vmem_spec,) * 3,
        scratch_shapes=[
            pltpu.VMEM(mask.shape, jnp.int32),
            pltpu.VMEM((nh, 2, 768, 128), bf16),
            pltpu.VMEM((nh, 2, 256, 128), bf16),
            pltpu.VMEM((6, 5, heads, 128), f32),
            pltpu.VMEM((nh, 256, 768), f32),
            pltpu.VMEM((nh, 256, 768), f32),
            pltpu.VMEM((256, 768), bf16),
            pltpu.VMEM((256, 768), bf16),
            pltpu.VMEM((3, nh, 8, 128), f32),
            pltpu.VMEM((2, nh, 8, 128), f32),
            pltpu.VMEM((nh, 8, 128), f32),
            pltpu.VMEM((2, nh, 8, 128), f32),
            pltpu.VMEM((nh, 128, 256), f32),
            pltpu.VMEM((2, nh, 128, 256), bf16),
            pltpu.VMEM((2, nh, 128, 256), bf16),
            pltpu.VMEM((3, nh, 256, 128), bf16),
            dma((nh, 3)),
            dma((nh,)),
            dma((2, nh)),
            dma((2, nh)),
            dma((2, nh)),
            dma((2, 2)),
            dma((4,)),
            dma((2,)),
            dma((2,)),
            dma((2,)),
            dma((3,)),
            dma((3,)),
            dma,
        ],
        compiler_params=pltpu.CompilerParams(
            collective_id=0, has_side_effects=True, vmem_limit_bytes=53000 * 1024
        ),
        name="block_attention",
    )(*args, mask)
    result = pl.pallas_call(
        store,
        out_shape=(out, out, out),
        in_specs=[vmem_spec] * 3,
        out_specs=(hbm_spec,) * 3,
        scratch_shapes=[dma((3,))],
        compiler_params=pltpu.CompilerParams(vmem_limit_bytes=4 * 1024 * 1024),
        name="store_gradients",
    )(*result)
    return tuple(jnp.transpose(x, (1, 0, 2)) for x in result)


def solution(mesh):
    spec = P(("dp", "seq"), None, None)
    return jax.shard_map(
        functools.partial(per_device, seq_size=mesh.shape["seq"]),
        mesh=mesh,
        in_specs=(spec, spec, spec, spec, P()),
        out_specs=(spec, spec, spec),
        check_vma=False,
    )
```

```python
import functools
import math

import jax
import jax.numpy as jnp
from jax import lax
from jax.experimental import pallas as pl
from jax.experimental.pallas import tpu as pltpu
from jax.sharding import PartitionSpec as P

NEG = -1e30
AHEAD = 2
LAG_TOTAL = 3
LAG_GRAD = 6
LAG_OUT = 9

NT = (((1,), (1,)), ((), ()))
NN = (((1,), (0,)), ((), ()))


def dot(a, b, dims):
    return lax.dot_general(a, b, dims, preferred_element_type=jnp.float32)


def kernel(
    seq_size,
    heads,
    scale,
    q_hbm,
    k_hbm,
    v_hbm,
    g_hbm,
    mask_hbm,
    dq_out,
    dk_out,
    dv_out,
    mask_ref,
    qg,
    kv,
    bias,
    exps,
    dps,
    w_ref,
    ds_ref,
    peaks,
    part,
    part_in,
    tot,
    tot_in,
    dq_own,
    dq_pass,
    dq_send,
    dq_in,
    obuf,
    recv_qg,
    recv_kv,
    recv_part,
    recv_tot,
    recv_dq,
    recv_pass,
    send_far,
    send_near,
    send_part,
    send_tot,
    send_dq,
    send_pass,
    out_send,
    out_recv,
    mask_sem,
):
    nh = heads // 2
    me = lax.axis_index("seq")
    core = lax.rem(me, 2)
    other = 1 - core
    first = me - core
    left = first - 2
    right = first + 2
    has_left = first > 0
    has_right = right < seq_size
    sibling = first + other
    left_mate = left + core
    right_mate = right + core
    mine = pl.ds(pl.multiple_of(core * 128, 128), 128)
    theirs = pl.ds(pl.multiple_of(other * 128, 128), 128)

    barrier = pltpu.get_barrier_semaphore()

    def greet(to):
        pl.semaphore_signal(barrier, inc=1, device_id={"seq": to}, device_id_type=pl.DeviceIdType.MESH)

    greet(sibling)
    for side, base, present in ((0, left, has_left), (1, right, has_right)):

        @pl.when(present)
        def _():
            greet(base)
            greet(base + 1)

    mask_copy = pltpu.make_async_copy(mask_hbm, mask_ref, mask_sem)
    mask_copy.start()

    def remote(src, dst, send, recv, to):
        return pltpu.make_async_remote_copy(
            src_ref=src,
            dst_ref=dst,
            send_sem=send,
            recv_sem=recv,
            device_id={"seq": to},
            device_id_type=pl.DeviceIdType.MESH,
        )

    def wait_for(ref, sem):
        pltpu.make_async_copy(ref, ref, sem).wait()

    def span(s, c):
        return pl.ds(pl.multiple_of(s * 256 + c * 128, 128), 128)

    def to_mate(s, src, dst, send, recv, h):
        side = s // 2
        mate = right_mate if side else left_mate
        remote(src, dst.at[1 - side, h], send.at[side], recv.at[1 - side, h], mate).start()

    def load_own(h):
        src = core * nh + h
        pltpu.make_async_copy(q_hbm.at[src], qg.at[h, 0, span(1, core)], recv_qg.at[h, 1]).start()
        pltpu.make_async_copy(g_hbm.at[src], qg.at[h, 1, span(1, core)], recv_qg.at[h, 1]).start()
        pltpu.make_async_copy(k_hbm.at[src], kv.at[h, 0, mine], recv_kv.at[h]).start()
        pltpu.make_async_copy(v_hbm.at[src], kv.at[h, 1, mine], recv_kv.at[h]).start()

    def send_head(h):
        away = other * nh + h
        own_span = span(1, core)
        remote(q_hbm.at[away], qg.at[h, 0, own_span], send_near.at[0], recv_qg.at[h, 1], sibling).start()
        remote(g_hbm.at[away], qg.at[h, 1, own_span], send_near.at[1], recv_qg.at[h, 1], sibling).start()
        remote(k_hbm.at[away], kv.at[h, 0, mine], send_near.at[2], recv_kv.at[h], sibling).start()
        remote(v_hbm.at[away], kv.at[h, 1, mine], send_near.at[3], recv_kv.at[h], sibling).start()
        for side, base, present in ((0, left, has_left), (1, right, has_right)):
            slot = 2 - 2 * side

            @pl.when(present)
            def _():
                for half in range(2):
                    src = half * nh + h
                    to = base + half
                    remote(
                        q_hbm.at[src], qg.at[h, 0, span(slot, core)], send_far.at[side, 0], recv_qg.at[h, slot], to
                    ).start()
                    remote(
                        g_hbm.at[src], qg.at[h, 1, span(slot, core)], send_far.at[side, 1], recv_qg.at[h, slot], to
                    ).start()

    for h in range(nh):
        load_own(h)
    zero = jnp.zeros((128, 128), jnp.bfloat16)
    for ref in (w_ref, ds_ref):
        ref[128:256, 0:128] = zero
        ref[0:128, 640:768] = zero

    pl.semaphore_wait(barrier, 1 + 2 * has_left.astype(jnp.int32) + 2 * has_right.astype(jnp.int32))

    for h in range(AHEAD):
        send_head(h)

    mask_copy.wait()
    planes = mask_ref[...]
    block_at = lax.broadcasted_iota(jnp.int32, planes.shape, 2)
    for t in range(6):
        picked = jnp.where(block_at == first - 2 + t, planes, 0)
        allowed = jnp.max(picked, axis=2, keepdims=True)
        bias[t] = jnp.broadcast_to(jnp.where(allowed > 0, 0.0, NEG), bias.shape[1:])
    for side, present in ((0, has_left), (1, has_right)):

        @pl.when(jnp.logical_not(present))
        def _():
            edge = slice(512 * side, 512 * side + 256)
            qg[:, :, edge, :] = jnp.zeros((nh, 2, 256, 128), jnp.bfloat16)
            part_in[side, :, 0:2, :] = jnp.full((nh, 2, 128), NEG, jnp.float32)
            part_in[side, :, 2:4, :] = jnp.zeros((nh, 2, 128), jnp.float32)
            tot_in[side] = jnp.zeros(tot_in.shape[1:], jnp.float32)
            dq_in[side] = jnp.zeros(dq_in.shape[1:], jnp.bfloat16)

    log_scale = scale * math.log2(math.e)

    def on_side(s, act):
        if s == 1:
            act()
        else:
            pl.when(has_left if s == 0 else has_right)(act)

    def key_blocks(t):
        return (0,) if t == 0 else (1,) if t == 5 else (0, 1)

    def scores(h):
        wait_for(kv.at[h], recv_kv.at[h])
        keys = kv[h, 0]
        values = kv[h, 1]
        for s in (1, 0, 2):
            on_side(s, lambda: wait_for(qg.at[h, :, s * 256 : s * 256 + 256], recv_qg.at[h, s]))
            raw = dot(keys, qg[h, 0, s * 256 : s * 256 + 256], NT)
            dp = dot(values, qg[h, 1, s * 256 : s * 256 + 256], NT)
            for a in range(2):
                t = 2 * s + a
                cols = slice(a * 128, a * 128 + 128)
                put = slice(t * 128, t * 128 + 128)
                logits = {}
                for b in key_blocks(t):
                    row = bias[t, b + 4 - t, pl.ds(core * nh + h, 1), :]
                    logits[b] = raw[b * 128 : b * 128 + 128, cols] * log_scale + row
                peak = functools.reduce(
                    jnp.maximum, [jnp.max(x, axis=0, keepdims=True) for x in logits.values()]
                )
                total = 0.0
                delta = 0.0
                for b, x in logits.items():
                    rows = slice(b * 128, b * 128 + 128)
                    e = jnp.exp2(x - peak)
                    g = dp[rows, cols]
                    exps[h, rows, put] = e
                    dps[h, rows, put] = g
                    total = total + jnp.sum(e, axis=0, keepdims=True)
                    delta = delta + jnp.sum(e * g, axis=0, keepdims=True)
                peaks[s, h, a : a + 1, :] = peak
                part[s, h, a : a + 1, :] = peak + jnp.log2(total)
                part[s, h, 2 + a : 3 + a, :] = delta / total
            if s != 1:
                on_side(s, lambda: to_mate(s, part.at[s, h], part_in, send_part, recv_part, h))

    def totals(h):
        for s in (0, 2):
            on_side(s, lambda: wait_for(part_in.at[s // 2, h], recv_part.at[s // 2, h]))
        tiles = [part[1, h], part_in[0, h], part_in[1, h]]
        peak = functools.reduce(jnp.maximum, [x[0:2] for x in tiles])
        total = 0.0
        delta = 0.0
        for x in tiles:
            f = jnp.exp2(x[0:2] - peak)
            total = total + f
            delta = delta + x[2:4] * f
        tot[h, 0:2, :] = peak + jnp.log2(total)
        tot[h, 2:4, :] = delta / total
        for s in (0, 2):
            on_side(s, lambda: to_mate(s, tot.at[h], tot_in, send_tot, recv_tot, h))

    def give(h, which, out, value):
        value = value.astype(jnp.bfloat16)
        obuf[which, h] = value
        out[core * nh + h] = obuf[which, h, mine]
        remote(
            obuf.at[which, h, theirs], out.at[core * nh + h], out_send.at[which], out_recv.at[which], sibling
        ).start()

    def grads(h):
        for s in (0, 2):
            on_side(s, lambda: wait_for(tot_in.at[s // 2, h], recv_tot.at[s // 2, h]))
        tiles = [tot_in[0, h], tot[h], tot_in[1, h]]
        for t in range(6):
            s, a = divmod(t, 2)
            put = slice(t * 128, t * 128 + 128)
            tile = tiles[s]
            f = jnp.exp2(peaks[s, h, a : a + 1, :] - tile[a : a + 1])
            shift = tile[2 + a : 3 + a]
            for b in key_blocks(t):
                rows = slice(b * 128, b * 128 + 128)
                w = exps[h, rows, put] * f
                w_ref[rows, put] = w.astype(jnp.bfloat16)
                ds_ref[rows, put] = (w * (dps[h, rows, put] - shift)).astype(jnp.bfloat16)
        ds = ds_ref[...]
        dq = dot(kv[h, 0].T, ds, NN)
        head = core * nh + h
        for side, base, present in ((0, left, has_left), (1, right, has_right)):
            for a in range(2):
                t = 4 * side + a
                dq_send[side, h, a] = dq[:, t * 128 : t * 128 + 128].astype(jnp.bfloat16)

            @pl.when(present)
            def _():
                for a in range(2):
                    remote(
                        dq_send.at[side, h, a],
                        dq_in.at[1 - side, head],
                        send_dq.at[side],
                        recv_dq.at[1 - side, head],
                        base + a,
                    ).start()

        dq_own[head] = jnp.where(core == 0, dq[:, 256:384], dq[:, 384:512])
        dq_pass[h] = jnp.where(core == 0, dq[:, 384:512], dq[:, 256:384])
        remote(dq_pass.at[h], dq_own.at[head], send_pass, recv_pass.at[h], sibling).start()
        give(h, 0, dk_out, dot(ds, qg[h, 0], NN) * scale)
        give(h, 1, dv_out, dot(w_ref[...], qg[h, 1], NN))

    def outputs(h):
        wait_for(dq_own.at[other * nh + h], recv_pass.at[h])
        for g in (h, nh + h):
            for s in (0, 2):
                on_side(s, lambda: wait_for(dq_in.at[s // 2, g], recv_dq.at[s // 2, g]))
            dq = dq_own[g] + dq_in[0, g].astype(jnp.float32) + dq_in[1, g].astype(jnp.float32)
            dq_out[g] = (dq * scale).T.astype(jnp.bfloat16)

    def step(i, carry):
        @pl.when(i + AHEAD < nh)
        def _():
            send_head(i + AHEAD)

        @pl.when((i >= LAG_TOTAL) & (i < nh + LAG_TOTAL))
        def _():
            totals(i - LAG_TOTAL)

        @pl.when((i >= LAG_GRAD) & (i < nh + LAG_GRAD))
        def _():
            grads(i - LAG_GRAD)

        @pl.when(i >= LAG_OUT)
        def _():
            outputs(i - LAG_OUT)

        @pl.when(i < nh)
        def _():
            scores(i)

        return carry

    lax.fori_loop(0, nh + LAG_OUT, step, 0)

    for side, present in ((0, has_left), (1, has_right)):

        @pl.when(present)
        def _():
            wait_for(q_hbm, send_far.at[side, 0])
            wait_for(g_hbm, send_far.at[side, 1])
            wait_for(part.at[0], send_part.at[side])
            wait_for(tot, send_tot.at[side])
            wait_for(dq_send.at[side], send_dq.at[side])

    for which, ref in enumerate((q_hbm, g_hbm, k_hbm, v_hbm)):
        wait_for(ref.at[0:nh], send_near.at[which])
    wait_for(dq_pass, send_pass)
    for which, ref in enumerate((dk_out, dv_out)):
        half = ref.at[0:nh]
        wait_for(half, out_send.at[which])
        wait_for(half, out_recv.at[which])


def store(dq_ref, dk_ref, dv_ref, dq_hbm, dk_hbm, dv_hbm, sem):
    copies = [
        pltpu.make_async_copy(src, dst, sem.at[i])
        for i, (src, dst) in enumerate(((dq_ref, dq_hbm), (dk_ref, dk_hbm), (dv_ref, dv_hbm)))
    ]
    for copy in copies:
        copy.start()
    for copy in copies:
        copy.wait()


def in_hbm(x):
    return pltpu.with_memory_space_constraint(x, pltpu.HBM)


def per_device(queries, keys, values, out_grad, block_mask, seq_size):
    tokens, heads, width = queries.shape
    nh = heads // 2
    args = [in_hbm(jnp.transpose(x, (1, 0, 2))) for x in (queries, keys, values, out_grad)]
    mask = in_hbm(jnp.transpose(block_mask, (2, 0, 1)))
    out = jax.ShapeDtypeStruct((heads, tokens, width), jnp.bfloat16)
    bf16, f32 = jnp.bfloat16, jnp.float32
    dma = pltpu.SemaphoreType.DMA
    hbm_spec = pl.BlockSpec(memory_space=pltpu.HBM)
    vmem_spec = pl.BlockSpec(memory_space=pltpu.VMEM)
    result = pl.pallas_call(
        functools.partial(kernel, seq_size, heads, 1.0 / math.sqrt(width)),
        out_shape=(out, out, out),
        in_specs=[hbm_spec] * 5,
        out_specs=(vmem_spec,) * 3,
        scratch_shapes=[
            pltpu.VMEM(mask.shape, jnp.int32),
            pltpu.VMEM((nh, 2, 768, 128), bf16),
            pltpu.VMEM((nh, 2, 256, 128), bf16),
            pltpu.VMEM((6, 5, heads, 128), f32),
            pltpu.VMEM((nh, 256, 768), f32),
            pltpu.VMEM((nh, 256, 768), f32),
            pltpu.VMEM((256, 768), bf16),
            pltpu.VMEM((256, 768), bf16),
            pltpu.VMEM((3, nh, 2, 128), f32),
            pltpu.VMEM((3, nh, 4, 128), f32),
            pltpu.VMEM((2, nh, 4, 128), f32),
            pltpu.VMEM((nh, 4, 128), f32),
            pltpu.VMEM((2, nh, 4, 128), f32),
            pltpu.VMEM((heads, 128, 128), f32),
            pltpu.VMEM((nh, 128, 128), f32),
            pltpu.VMEM((2, nh, 2, 128, 128), bf16),
            pltpu.VMEM((2, heads, 128, 128), bf16),
            pltpu.VMEM((2, nh, 256, 128), bf16),
            dma((nh, 3)),
            dma((nh,)),
            dma((2, nh)),
            dma((2, nh)),
            dma((2, heads)),
            dma((nh,)),
            dma((2, 2)),
            dma((4,)),
            dma((2,)),
            dma((2,)),
            dma((2,)),
            dma,
            dma((2,)),
            dma((2,)),
            dma,
        ],
        compiler_params=pltpu.CompilerParams(
            collective_id=0, has_side_effects=True, vmem_limit_bytes=48000 * 1024
        ),
        name="block_attention",
    )(*args, mask)
    result = pl.pallas_call(
        store,
        out_shape=(out, out, out),
        in_specs=[vmem_spec] * 3,
        out_specs=(hbm_spec,) * 3,
        scratch_shapes=[dma((3,))],
        compiler_params=pltpu.CompilerParams(vmem_limit_bytes=4 * 1024 * 1024),
        name="store_gradients",
    )(*result)
    return tuple(jnp.transpose(x, (1, 0, 2)) for x in result)


def solution(mesh):
    spec = P(("dp", "seq"), None, None)
    return jax.shard_map(
        functools.partial(per_device, seq_size=mesh.shape["seq"]),
        mesh=mesh,
        in_specs=(spec, spec, spec, spec, P()),
        out_specs=(spec, spec, spec),
        check_vma=False,
    )
```

```python
import functools
import math

import jax
import jax.numpy as jnp
from jax import lax
from jax.experimental import pallas as pl
from jax.experimental.pallas import tpu as pltpu
from jax.sharding import PartitionSpec as P

NEG = -1e30
AHEAD = 2
LAG_TOTAL = 4
LAG_GRAD = 7
LAG_OUT = 11

NT = (((1,), (1,)), ((), ()))
NN = (((1,), (0,)), ((), ()))


def dot(a, b, dims):
    return lax.dot_general(a, b, dims, preferred_element_type=jnp.float32)


def kernel(
    seq_size,
    heads,
    scale,
    q_hbm,
    k_hbm,
    v_hbm,
    g_hbm,
    mask_hbm,
    dq_out,
    dk_out,
    dv_out,
    mask_ref,
    qg,
    kv,
    bias,
    exps,
    dps,
    w_ref,
    ds_ref,
    peaks,
    part,
    part_in,
    tot,
    tot_in,
    dq_own,
    dq_pass,
    dq_send,
    dq_in,
    obuf,
    recv_qg,
    recv_kv,
    recv_part,
    recv_tot,
    recv_dq,
    recv_pass,
    send_far,
    send_near,
    send_part,
    send_tot,
    send_dq,
    send_pass,
    out_send,
    out_recv,
    mask_sem,
    entered,
):
    nh = heads // 2
    me = lax.axis_index("seq")
    core = lax.rem(me, 2)
    other = 1 - core
    first = me - core
    left = first - 2
    right = first + 2
    has_left = first > 0
    has_right = right < seq_size
    sibling = first + other
    left_mate = left + core
    right_mate = right + core
    mine = pl.ds(pl.multiple_of(core * 128, 128), 128)
    theirs = pl.ds(pl.multiple_of(other * 128, 128), 128)

    barrier = pltpu.get_barrier_semaphore()

    def greet(sem, to):
        pl.semaphore_signal(sem, inc=1, device_id={"seq": to}, device_id_type=pl.DeviceIdType.MESH)

    part_zero = lax.axis_index("dp") == 0
    enters_last = part_zero & (me == 0)
    meets_last = part_zero & (me > 0) & (me < 4)

    @pl.when(jnp.logical_not(enters_last))
    def _():
        greet(barrier, sibling)
        for base, present in ((left, has_left), (right, has_right)):

            @pl.when(present)
            def _():
                greet(barrier, base)
                greet(barrier, base + 1)

    mask_copy = pltpu.make_async_copy(mask_hbm, mask_ref, mask_sem)
    mask_copy.start()

    def remote(src, dst, send, recv, to):
        return pltpu.make_async_remote_copy(
            src_ref=src,
            dst_ref=dst,
            send_sem=send,
            recv_sem=recv,
            device_id={"seq": to},
            device_id_type=pl.DeviceIdType.MESH,
        )

    def wait_for(ref, sem):
        pltpu.make_async_copy(ref, ref, sem).wait()

    def span(s, c):
        return pl.ds(pl.multiple_of(s * 256 + c * 128, 128), 128)

    def to_mate(s, src, dst, send, recv, h):
        side = s // 2
        mate = right_mate if side else left_mate
        remote(src, dst.at[1 - side, h], send.at[side], recv.at[1 - side, h], mate).start()

    def load_own(h):
        src = core * nh + h
        pltpu.make_async_copy(q_hbm.at[src], qg.at[h, 0, span(1, core)], recv_qg.at[h, 1]).start()
        pltpu.make_async_copy(g_hbm.at[src], qg.at[h, 1, span(1, core)], recv_qg.at[h, 1]).start()
        pltpu.make_async_copy(k_hbm.at[src], kv.at[h, 0, mine], recv_kv.at[h]).start()
        pltpu.make_async_copy(v_hbm.at[src], kv.at[h, 1, mine], recv_kv.at[h]).start()

    def send_near_head(h):
        away = other * nh + h
        own_span = span(1, core)
        remote(q_hbm.at[away], qg.at[h, 0, own_span], send_near.at[0], recv_qg.at[h, 1], sibling).start()
        remote(g_hbm.at[away], qg.at[h, 1, own_span], send_near.at[1], recv_qg.at[h, 1], sibling).start()
        remote(k_hbm.at[away], kv.at[h, 0, mine], send_near.at[2], recv_kv.at[h], sibling).start()
        remote(v_hbm.at[away], kv.at[h, 1, mine], send_near.at[3], recv_kv.at[h], sibling).start()

    def send_far_head(h, side, half):
        src = half * nh + h
        slot = 2 - 2 * side
        to = (right if side else left) + half
        place = span(slot, core)
        remote(q_hbm.at[src], qg.at[h, 0, place], send_far.at[side, 0], recv_qg.at[h, slot], to).start()
        remote(g_hbm.at[src], qg.at[h, 1, place], send_far.at[side, 1], recv_qg.at[h, slot], to).start()

    def send_head(h):
        send_near_head(h)
        for side, present in ((0, has_left), (1, has_right)):

            @pl.when(present)
            def _():
                for half in range(2):
                    send_far_head(h, side, half)

    def send_head_early(h):
        pl.when(jnp.logical_not(meets_last & (me == 1)))(lambda: send_near_head(h))
        pl.when(has_left & jnp.logical_not(meets_last))(lambda: send_far_head(h, 0, 0))
        pl.when(has_left)(lambda: send_far_head(h, 0, 1))

        @pl.when(has_right)
        def _():
            for half in range(2):
                send_far_head(h, 1, half)

    def send_head_late(h):
        pl.when(me == 1)(lambda: send_near_head(h))
        pl.when(me > 1)(lambda: send_far_head(h, 0, 0))

    for h in range(nh):
        load_own(h)
    zero = jnp.zeros((128, 128), jnp.bfloat16)
    for ref in (w_ref, ds_ref):
        ref[128:256, 0:128] = zero
        ref[0:128, 640:768] = zero

    early = 1 + 2 * has_left.astype(jnp.int32) + 2 * has_right.astype(jnp.int32) - meets_last.astype(jnp.int32)
    pl.semaphore_wait(barrier, early)

    @pl.when(enters_last)
    def _():
        for to in (sibling, right, right + 1):
            greet(entered, to)


    for h in range(AHEAD):
        send_head_early(h)

    @pl.when(meets_last)
    def _():
        pl.semaphore_wait(entered, 1)
        for h in range(AHEAD):
            send_head_late(h)

    mask_copy.wait()
    planes = mask_ref[...]
    block_at = lax.broadcasted_iota(jnp.int32, planes.shape, 2)
    for t in range(6):
        picked = jnp.where(block_at == first - 2 + t, planes, 0)
        allowed = jnp.max(picked, axis=2, keepdims=True)
        bias[t] = jnp.broadcast_to(jnp.where(allowed > 0, 0.0, NEG), bias.shape[1:])
    for side, present in ((0, has_left), (1, has_right)):

        @pl.when(jnp.logical_not(present))
        def _():
            edge = slice(512 * side, 512 * side + 256)
            qg[:, :, edge, :] = jnp.zeros((nh, 2, 256, 128), jnp.bfloat16)
            part_in[side, :, 0:2, :] = jnp.full((nh, 2, 128), NEG, jnp.float32)
            part_in[side, :, 2:4, :] = jnp.zeros((nh, 2, 128), jnp.float32)
            tot_in[side] = jnp.zeros(tot_in.shape[1:], jnp.float32)
            dq_in[side] = jnp.zeros(dq_in.shape[1:], jnp.bfloat16)

    log_scale = scale * math.log2(math.e)

    def on_side(s, act):
        if s == 1:
            act()
        else:
            pl.when(has_left if s == 0 else has_right)(act)

    def key_blocks(t):
        return (0,) if t == 0 else (1,) if t == 5 else (0, 1)

    def scores(h):
        wait_for(kv.at[h], recv_kv.at[h])
        keys = kv[h, 0]
        values = kv[h, 1]
        for s in (1, 0, 2):
            on_side(s, lambda: wait_for(qg.at[h, :, s * 256 : s * 256 + 256], recv_qg.at[h, s]))
            raw = dot(keys, qg[h, 0, s * 256 : s * 256 + 256], NT)
            dp = dot(values, qg[h, 1, s * 256 : s * 256 + 256], NT)
            for a in range(2):
                t = 2 * s + a
                cols = slice(a * 128, a * 128 + 128)
                put = slice(t * 128, t * 128 + 128)
                logits = {}
                for b in key_blocks(t):
                    row = bias[t, b + 4 - t, pl.ds(core * nh + h, 1), :]
                    logits[b] = raw[b * 128 : b * 128 + 128, cols] * log_scale + row
                peak = functools.reduce(
                    jnp.maximum, [jnp.max(x, axis=0, keepdims=True) for x in logits.values()]
                )
                total = 0.0
                delta = 0.0
                for b, x in logits.items():
                    rows = slice(b * 128, b * 128 + 128)
                    e = jnp.exp2(x - peak)
                    g = dp[rows, cols]
                    exps[h, rows, put] = e
                    dps[h, rows, put] = g
                    total = total + jnp.sum(e, axis=0, keepdims=True)
                    delta = delta + jnp.sum(e * g, axis=0, keepdims=True)
                peaks[s, h, a : a + 1, :] = peak
                part[s, h, a : a + 1, :] = peak + jnp.log2(total)
                part[s, h, 2 + a : 3 + a, :] = delta / total
            if s != 1:
                on_side(s, lambda: to_mate(s, part.at[s, h], part_in, send_part, recv_part, h))

    def totals(h):
        for s in (0, 2):
            on_side(s, lambda: wait_for(part_in.at[s // 2, h], recv_part.at[s // 2, h]))
        tiles = [part[1, h], part_in[0, h], part_in[1, h]]
        peak = functools.reduce(jnp.maximum, [x[0:2] for x in tiles])
        total = 0.0
        delta = 0.0
        for x in tiles:
            f = jnp.exp2(x[0:2] - peak)
            total = total + f
            delta = delta + x[2:4] * f
        tot[h, 0:2, :] = peak + jnp.log2(total)
        tot[h, 2:4, :] = delta / total
        for s in (0, 2):
            on_side(s, lambda: to_mate(s, tot.at[h], tot_in, send_tot, recv_tot, h))

    def give(h, which, out, value):
        value = value.astype(jnp.bfloat16)
        obuf[which, h] = value
        out[core * nh + h] = obuf[which, h, mine]
        remote(
            obuf.at[which, h, theirs], out.at[core * nh + h], out_send.at[which], out_recv.at[which], sibling
        ).start()

    def grads(h):
        for s in (0, 2):
            on_side(s, lambda: wait_for(tot_in.at[s // 2, h], recv_tot.at[s // 2, h]))
        tiles = [tot_in[0, h], tot[h], tot_in[1, h]]
        for t in range(6):
            s, a = divmod(t, 2)
            put = slice(t * 128, t * 128 + 128)
            tile = tiles[s]
            f = jnp.exp2(peaks[s, h, a : a + 1, :] - tile[a : a + 1])
            shift = tile[2 + a : 3 + a]
            for b in key_blocks(t):
                rows = slice(b * 128, b * 128 + 128)
                w = exps[h, rows, put] * f
                w_ref[rows, put] = w.astype(jnp.bfloat16)
                ds_ref[rows, put] = (w * (dps[h, rows, put] - shift)).astype(jnp.bfloat16)
        ds = ds_ref[...]
        dq = dot(kv[h, 0].T, ds, NN)
        head = core * nh + h
        for side, base, present in ((0, left, has_left), (1, right, has_right)):
            for a in range(2):
                t = 4 * side + a
                dq_send[side, h, a] = dq[:, t * 128 : t * 128 + 128].astype(jnp.bfloat16)

            @pl.when(present)
            def _():
                for a in range(2):
                    remote(
                        dq_send.at[side, h, a],
                        dq_in.at[1 - side, head],
                        send_dq.at[side],
                        recv_dq.at[1 - side, head],
                        base + a,
                    ).start()

        dq_own[head] = jnp.where(core == 0, dq[:, 256:384], dq[:, 384:512])
        dq_pass[h] = jnp.where(core == 0, dq[:, 384:512], dq[:, 256:384])
        remote(dq_pass.at[h], dq_own.at[head], send_pass, recv_pass.at[h], sibling).start()
        give(h, 0, dk_out, dot(ds, qg[h, 0], NN) * scale)
        give(h, 1, dv_out, dot(w_ref[...], qg[h, 1], NN))

    def outputs(h):
        wait_for(dq_own.at[other * nh + h], recv_pass.at[h])
        for g in (h, nh + h):
            for s in (0, 2):
                on_side(s, lambda: wait_for(dq_in.at[s // 2, g], recv_dq.at[s // 2, g]))
            dq = dq_own[g] + dq_in[0, g].astype(jnp.float32) + dq_in[1, g].astype(jnp.float32)
            dq_out[g] = (dq * scale).T.astype(jnp.bfloat16)

    def step(i, carry):
        @pl.when(i + AHEAD < nh)
        def _():
            send_head(i + AHEAD)

        @pl.when((i >= LAG_TOTAL) & (i < nh + LAG_TOTAL))
        def _():
            totals(i - LAG_TOTAL)

        @pl.when((i >= LAG_GRAD) & (i < nh + LAG_GRAD))
        def _():
            grads(i - LAG_GRAD)

        @pl.when(i >= LAG_OUT)
        def _():
            outputs(i - LAG_OUT)

        @pl.when(i < nh)
        def _():
            scores(i)

        return carry

    lax.fori_loop(0, nh + LAG_OUT, step, 0)

    for side, present in ((0, has_left), (1, has_right)):

        @pl.when(present)
        def _():
            wait_for(q_hbm, send_far.at[side, 0])
            wait_for(g_hbm, send_far.at[side, 1])
            wait_for(part.at[0], send_part.at[side])
            wait_for(tot, send_tot.at[side])
            wait_for(dq_send.at[side], send_dq.at[side])

    for which, ref in enumerate((q_hbm, g_hbm, k_hbm, v_hbm)):
        wait_for(ref.at[0:nh], send_near.at[which])
    wait_for(dq_pass, send_pass)
    for which, ref in enumerate((dk_out, dv_out)):
        half = ref.at[0:nh]
        wait_for(half, out_send.at[which])
        wait_for(half, out_recv.at[which])


def store(dq_ref, dk_ref, dv_ref, dq_hbm, dk_hbm, dv_hbm, sem):
    copies = [
        pltpu.make_async_copy(src, dst, sem.at[i])
        for i, (src, dst) in enumerate(((dq_ref, dq_hbm), (dk_ref, dk_hbm), (dv_ref, dv_hbm)))
    ]
    for copy in copies:
        copy.start()
    for copy in copies:
        copy.wait()


def in_hbm(x):
    return pltpu.with_memory_space_constraint(x, pltpu.HBM)


def per_device(queries, keys, values, out_grad, block_mask, seq_size):
    tokens, heads, width = queries.shape
    nh = heads // 2
    args = [in_hbm(jnp.transpose(x, (1, 0, 2))) for x in (queries, keys, values, out_grad)]
    mask = in_hbm(jnp.transpose(block_mask, (2, 0, 1)))
    out = jax.ShapeDtypeStruct((heads, tokens, width), jnp.bfloat16)
    bf16, f32 = jnp.bfloat16, jnp.float32
    dma = pltpu.SemaphoreType.DMA
    hbm_spec = pl.BlockSpec(memory_space=pltpu.HBM)
    vmem_spec = pl.BlockSpec(memory_space=pltpu.VMEM)
    result = pl.pallas_call(
        functools.partial(kernel, seq_size, heads, 1.0 / math.sqrt(width)),
        out_shape=(out, out, out),
        in_specs=[hbm_spec] * 5,
        out_specs=(vmem_spec,) * 3,
        scratch_shapes=[
            pltpu.VMEM(mask.shape, jnp.int32),
            pltpu.VMEM((nh, 2, 768, 128), bf16),
            pltpu.VMEM((nh, 2, 256, 128), bf16),
            pltpu.VMEM((6, 5, heads, 128), f32),
            pltpu.VMEM((nh, 256, 768), f32),
            pltpu.VMEM((nh, 256, 768), f32),
            pltpu.VMEM((256, 768), bf16),
            pltpu.VMEM((256, 768), bf16),
            pltpu.VMEM((3, nh, 2, 128), f32),
            pltpu.VMEM((3, nh, 4, 128), f32),
            pltpu.VMEM((2, nh, 4, 128), f32),
            pltpu.VMEM((nh, 4, 128), f32),
            pltpu.VMEM((2, nh, 4, 128), f32),
            pltpu.VMEM((heads, 128, 128), f32),
            pltpu.VMEM((nh, 128, 128), f32),
            pltpu.VMEM((2, nh, 2, 128, 128), bf16),
            pltpu.VMEM((2, heads, 128, 128), bf16),
            pltpu.VMEM((2, nh, 256, 128), bf16),
            dma((nh, 3)),
            dma((nh,)),
            dma((2, nh)),
            dma((2, nh)),
            dma((2, heads)),
            dma((nh,)),
            dma((2, 2)),
            dma((4,)),
            dma((2,)),
            dma((2,)),
            dma((2,)),
            dma,
            dma((2,)),
            dma((2,)),
            dma,
            pltpu.SemaphoreType.REGULAR,
        ],
        compiler_params=pltpu.CompilerParams(
            collective_id=0, has_side_effects=True, vmem_limit_bytes=48000 * 1024
        ),
        name="block_attention",
    )(*args, mask)
    result = pl.pallas_call(
        store,
        out_shape=(out, out, out),
        in_specs=[vmem_spec] * 3,
        out_specs=(hbm_spec,) * 3,
        scratch_shapes=[dma((3,))],
        compiler_params=pltpu.CompilerParams(vmem_limit_bytes=4 * 1024 * 1024),
        name="store_gradients",
    )(*result)
    return tuple(jnp.transpose(x, (1, 0, 2)) for x in result)


def solution(mesh):
    spec = P(("dp", "seq"), None, None)
    return jax.shard_map(
        functools.partial(per_device, seq_size=mesh.shape["seq"]),
        mesh=mesh,
        in_specs=(spec, spec, spec, spec, P()),
        out_specs=(spec, spec, spec),
        check_vma=False,
    )
```

```python
import functools
import math

import jax
import jax.numpy as jnp
from jax import lax
from jax.experimental import pallas as pl
from jax.experimental.pallas import tpu as pltpu
from jax.sharding import PartitionSpec as P

NEG = -1e30
AHEAD = 2
LAG_TOTAL = 4
LAG_GRAD = 7
LAG_OUT = 11

NT = (((1,), (1,)), ((), ()))
NN = (((1,), (0,)), ((), ()))


def dot(a, b, dims):
    return lax.dot_general(a, b, dims, preferred_element_type=jnp.float32)


def kernel(
    seq_size,
    heads,
    scale,
    q_hbm,
    k_hbm,
    v_hbm,
    g_hbm,
    mask_hbm,
    dq_out,
    dk_out,
    dv_out,
    mask_ref,
    qg,
    kv,
    bias,
    exps,
    dps,
    w_ref,
    ds_ref,
    peaks,
    part,
    part_in,
    tot,
    tot_in,
    dq_own,
    dq_pass,
    dq_send,
    dq_in,
    obuf,
    recv_qg,
    recv_kv,
    recv_part,
    recv_tot,
    recv_dq,
    recv_pass,
    send_far,
    send_near,
    send_part,
    send_tot,
    send_dq,
    send_pass,
    out_send,
    out_recv,
    mask_sem,
    entered,
):
    nh = heads // 2
    me = lax.axis_index("seq")
    core = lax.rem(me, 2)
    other = 1 - core
    first = me - core
    left = first - 2
    right = first + 2
    has_left = first > 0
    has_right = right < seq_size
    sibling = first + other
    left_mate = left + core
    right_mate = right + core
    mine = pl.ds(pl.multiple_of(core * 128, 128), 128)
    theirs = pl.ds(pl.multiple_of(other * 128, 128), 128)

    barrier = pltpu.get_barrier_semaphore()

    def greet(sem, to):
        pl.semaphore_signal(sem, inc=1, device_id={"seq": to}, device_id_type=pl.DeviceIdType.MESH)

    part_zero = lax.axis_index("dp") == 0
    enters_last = part_zero & (me == 0)
    meets_last = part_zero & (me > 0) & (me < 4)

    @pl.when(jnp.logical_not(enters_last))
    def _():
        greet(barrier, sibling)
        for base, present in ((left, has_left), (right, has_right)):

            @pl.when(present)
            def _():
                greet(barrier, base)
                greet(barrier, base + 1)

    mask_copy = pltpu.make_async_copy(mask_hbm, mask_ref, mask_sem)
    mask_copy.start()

    def remote(src, dst, send, recv, to):
        return pltpu.make_async_remote_copy(
            src_ref=src,
            dst_ref=dst,
            send_sem=send,
            recv_sem=recv,
            device_id={"seq": to},
            device_id_type=pl.DeviceIdType.MESH,
        )

    def wait_for(ref, sem):
        pltpu.make_async_copy(ref, ref, sem).wait()

    def span(s, c):
        return pl.ds(pl.multiple_of(s * 256 + c * 128, 128), 128)

    def to_mate(s, src, dst, send, recv, h):
        side = s // 2
        mate = right_mate if side else left_mate
        remote(src, dst.at[1 - side, h], send.at[side], recv.at[1 - side, h], mate).start()

    def load_own(h):
        src = core * nh + h
        pltpu.make_async_copy(q_hbm.at[src], qg.at[h, 0, span(1, core)], recv_qg.at[h, 1]).start()
        pltpu.make_async_copy(g_hbm.at[src], qg.at[h, 1, span(1, core)], recv_qg.at[h, 1]).start()
        pltpu.make_async_copy(k_hbm.at[src], kv.at[h, 0, mine], recv_kv.at[h]).start()
        pltpu.make_async_copy(v_hbm.at[src], kv.at[h, 1, mine], recv_kv.at[h]).start()

    def send_near_head(h):
        away = other * nh + h
        own_span = span(1, core)
        remote(q_hbm.at[away], qg.at[h, 0, own_span], send_near.at[0], recv_qg.at[h, 1], sibling).start()
        remote(g_hbm.at[away], qg.at[h, 1, own_span], send_near.at[1], recv_qg.at[h, 1], sibling).start()
        remote(k_hbm.at[away], kv.at[h, 0, mine], send_near.at[2], recv_kv.at[h], sibling).start()
        remote(v_hbm.at[away], kv.at[h, 1, mine], send_near.at[3], recv_kv.at[h], sibling).start()

    def send_far_head(h, side, half):
        src = half * nh + h
        slot = 2 - 2 * side
        to = (right if side else left) + half
        place = span(slot, core)
        remote(q_hbm.at[src], qg.at[h, 0, place], send_far.at[side, 0], recv_qg.at[h, slot], to).start()
        remote(g_hbm.at[src], qg.at[h, 1, place], send_far.at[side, 1], recv_qg.at[h, slot], to).start()

    def send_head(h):
        for side, present in ((0, has_left), (1, has_right)):

            @pl.when(present)
            def _():
                for half in range(2):
                    send_far_head(h, side, half)

        send_near_head(h)

    def send_head_early(h):
        pl.when(jnp.logical_not(meets_last & (me == 1)))(lambda: send_near_head(h))
        pl.when(has_left & jnp.logical_not(meets_last))(lambda: send_far_head(h, 0, 0))
        pl.when(has_left)(lambda: send_far_head(h, 0, 1))

        @pl.when(has_right)
        def _():
            for half in range(2):
                send_far_head(h, 1, half)

    def send_head_late(h):
        pl.when(me == 1)(lambda: send_near_head(h))
        pl.when(me > 1)(lambda: send_far_head(h, 0, 0))

    for h in range(nh):
        load_own(h)
    zero = jnp.zeros((128, 128), jnp.bfloat16)
    for ref in (w_ref, ds_ref):
        ref[128:256, 0:128] = zero
        ref[0:128, 640:768] = zero

    early = 1 + 2 * has_left.astype(jnp.int32) + 2 * has_right.astype(jnp.int32) - meets_last.astype(jnp.int32)
    pl.semaphore_wait(barrier, early)

    @pl.when(enters_last)
    def _():
        for to in (sibling, right, right + 1):
            greet(entered, to)


    for h in range(AHEAD):
        send_head_early(h)

    @pl.when(meets_last)
    def _():
        pl.semaphore_wait(entered, 1)
        for h in range(AHEAD):
            send_head_late(h)

    mask_copy.wait()
    planes = mask_ref[...]
    block_at = lax.broadcasted_iota(jnp.int32, planes.shape, 2)
    for t in range(6):
        picked = jnp.where(block_at == first - 2 + t, planes, 0)
        allowed = jnp.max(picked, axis=2, keepdims=True)
        bias[t] = jnp.broadcast_to(jnp.where(allowed > 0, 0.0, NEG), bias.shape[1:])
    for side, present in ((0, has_left), (1, has_right)):

        @pl.when(jnp.logical_not(present))
        def _():
            edge = slice(512 * side, 512 * side + 256)
            qg[:, :, edge, :] = jnp.zeros((nh, 2, 256, 128), jnp.bfloat16)
            part_in[side, :, 0:2, :] = jnp.full((nh, 2, 128), NEG, jnp.float32)
            part_in[side, :, 2:4, :] = jnp.zeros((nh, 2, 128), jnp.float32)
            tot_in[side] = jnp.zeros(tot_in.shape[1:], jnp.float32)
            dq_in[side] = jnp.zeros(dq_in.shape[1:], jnp.bfloat16)

    log_scale = scale * math.log2(math.e)

    def on_side(s, act):
        if s == 1:
            act()
        else:
            pl.when(has_left if s == 0 else has_right)(act)

    def key_blocks(t):
        return (0,) if t == 0 else (1,) if t == 5 else (0, 1)

    def scores(h):
        wait_for(kv.at[h], recv_kv.at[h])
        keys = kv[h, 0]
        values = kv[h, 1]
        for s in (1, 0, 2):
            on_side(s, lambda: wait_for(qg.at[h, :, s * 256 : s * 256 + 256], recv_qg.at[h, s]))
            raw = dot(keys, qg[h, 0, s * 256 : s * 256 + 256], NT)
            dp = dot(values, qg[h, 1, s * 256 : s * 256 + 256], NT)
            for a in range(2):
                t = 2 * s + a
                cols = slice(a * 128, a * 128 + 128)
                put = slice(t * 128, t * 128 + 128)
                logits = {}
                for b in key_blocks(t):
                    row = bias[t, b + 4 - t, pl.ds(core * nh + h, 1), :]
                    logits[b] = raw[b * 128 : b * 128 + 128, cols] * log_scale + row
                peak = functools.reduce(
                    jnp.maximum, [jnp.max(x, axis=0, keepdims=True) for x in logits.values()]
                )
                total = 0.0
                delta = 0.0
                for b, x in logits.items():
                    rows = slice(b * 128, b * 128 + 128)
                    e = jnp.exp2(x - peak)
                    g = dp[rows, cols]
                    exps[h, rows, put] = e
                    dps[h, rows, put] = g
                    total = total + jnp.sum(e, axis=0, keepdims=True)
                    delta = delta + jnp.sum(e * g, axis=0, keepdims=True)
                peaks[s, h, a : a + 1, :] = peak
                part[s, h, a : a + 1, :] = peak + jnp.log2(total)
                part[s, h, 2 + a : 3 + a, :] = delta / total
            if s != 1:
                on_side(s, lambda: to_mate(s, part.at[s, h], part_in, send_part, recv_part, h))

    def totals(h):
        for s in (0, 2):
            on_side(s, lambda: wait_for(part_in.at[s // 2, h], recv_part.at[s // 2, h]))
        tiles = [part[1, h], part_in[0, h], part_in[1, h]]
        peak = functools.reduce(jnp.maximum, [x[0:2] for x in tiles])
        total = 0.0
        delta = 0.0
        for x in tiles:
            f = jnp.exp2(x[0:2] - peak)
            total = total + f
            delta = delta + x[2:4] * f
        tot[h, 0:2, :] = peak + jnp.log2(total)
        tot[h, 2:4, :] = delta / total
        for s in (0, 2):
            on_side(s, lambda: to_mate(s, tot.at[h], tot_in, send_tot, recv_tot, h))

    def give(h, which, out, value):
        value = value.astype(jnp.bfloat16)
        obuf[which, h] = value
        out[core * nh + h] = obuf[which, h, mine]
        remote(
            obuf.at[which, h, theirs], out.at[core * nh + h], out_send.at[which], out_recv.at[which], sibling
        ).start()

    def grads(h):
        for s in (0, 2):
            on_side(s, lambda: wait_for(tot_in.at[s // 2, h], recv_tot.at[s // 2, h]))
        tiles = [tot_in[0, h], tot[h], tot_in[1, h]]
        for t in range(6):
            s, a = divmod(t, 2)
            put = slice(t * 128, t * 128 + 128)
            tile = tiles[s]
            f = jnp.exp2(peaks[s, h, a : a + 1, :] - tile[a : a + 1])
            shift = tile[2 + a : 3 + a]
            for b in key_blocks(t):
                rows = slice(b * 128, b * 128 + 128)
                w = exps[h, rows, put] * f
                w_ref[rows, put] = w.astype(jnp.bfloat16)
                ds_ref[rows, put] = (w * (dps[h, rows, put] - shift)).astype(jnp.bfloat16)
        ds = ds_ref[...]
        dq = dot(kv[h, 0].T, ds, NN)
        head = core * nh + h
        for side, base, present in ((0, left, has_left), (1, right, has_right)):
            for a in range(2):
                t = 4 * side + a
                dq_send[side, h, a] = dq[:, t * 128 : t * 128 + 128].astype(jnp.bfloat16)

            @pl.when(present)
            def _():
                for a in range(2):
                    remote(
                        dq_send.at[side, h, a],
                        dq_in.at[1 - side, head],
                        send_dq.at[side],
                        recv_dq.at[1 - side, head],
                        base + a,
                    ).start()

        dq_own[head] = jnp.where(core == 0, dq[:, 256:384], dq[:, 384:512])
        dq_pass[h] = jnp.where(core == 0, dq[:, 384:512], dq[:, 256:384])
        remote(dq_pass.at[h], dq_own.at[head], send_pass, recv_pass.at[h], sibling).start()
        give(h, 0, dk_out, dot(ds, qg[h, 0], NN) * scale)
        give(h, 1, dv_out, dot(w_ref[...], qg[h, 1], NN))

    def outputs(h):
        wait_for(dq_own.at[other * nh + h], recv_pass.at[h])
        for g in (h, nh + h):
            for s in (0, 2):
                on_side(s, lambda: wait_for(dq_in.at[s // 2, g], recv_dq.at[s // 2, g]))
            dq = dq_own[g] + dq_in[0, g].astype(jnp.float32) + dq_in[1, g].astype(jnp.float32)
            dq_out[g] = (dq * scale).T.astype(jnp.bfloat16)

    def step(i, carry):
        @pl.when((i >= LAG_TOTAL) & (i < nh + LAG_TOTAL))
        def _():
            totals(i - LAG_TOTAL)

        @pl.when(i + AHEAD < nh)
        def _():
            send_head(i + AHEAD)

        @pl.when((i >= LAG_GRAD) & (i < nh + LAG_GRAD))
        def _():
            grads(i - LAG_GRAD)

        @pl.when(i >= LAG_OUT)
        def _():
            outputs(i - LAG_OUT)

        @pl.when(i < nh)
        def _():
            scores(i)

        return carry

    lax.fori_loop(0, nh + LAG_OUT, step, 0)

    for side, present in ((0, has_left), (1, has_right)):

        @pl.when(present)
        def _():
            wait_for(q_hbm, send_far.at[side, 0])
            wait_for(g_hbm, send_far.at[side, 1])
            wait_for(part.at[0], send_part.at[side])
            wait_for(tot, send_tot.at[side])
            wait_for(dq_send.at[side], send_dq.at[side])

    for which, ref in enumerate((q_hbm, g_hbm, k_hbm, v_hbm)):
        wait_for(ref.at[0:nh], send_near.at[which])
    wait_for(dq_pass, send_pass)
    for which, ref in enumerate((dk_out, dv_out)):
        half = ref.at[0:nh]
        wait_for(half, out_send.at[which])
        wait_for(half, out_recv.at[which])


def store(dq_ref, dk_ref, dv_ref, dq_hbm, dk_hbm, dv_hbm, sem):
    copies = [
        pltpu.make_async_copy(src, dst, sem.at[i])
        for i, (src, dst) in enumerate(((dq_ref, dq_hbm), (dk_ref, dk_hbm), (dv_ref, dv_hbm)))
    ]
    for copy in copies:
        copy.start()
    for copy in copies:
        copy.wait()


def in_hbm(x):
    return pltpu.with_memory_space_constraint(x, pltpu.HBM)


def per_device(queries, keys, values, out_grad, block_mask, seq_size):
    tokens, heads, width = queries.shape
    nh = heads // 2
    args = [in_hbm(jnp.transpose(x, (1, 0, 2))) for x in (queries, keys, values, out_grad)]
    mask = in_hbm(jnp.transpose(block_mask, (2, 0, 1)))
    out = jax.ShapeDtypeStruct((heads, tokens, width), jnp.bfloat16)
    bf16, f32 = jnp.bfloat16, jnp.float32
    dma = pltpu.SemaphoreType.DMA
    hbm_spec = pl.BlockSpec(memory_space=pltpu.HBM)
    vmem_spec = pl.BlockSpec(memory_space=pltpu.VMEM)
    result = pl.pallas_call(
        functools.partial(kernel, seq_size, heads, 1.0 / math.sqrt(width)),
        out_shape=(out, out, out),
        in_specs=[hbm_spec] * 5,
        out_specs=(vmem_spec,) * 3,
        scratch_shapes=[
            pltpu.VMEM(mask.shape, jnp.int32),
            pltpu.VMEM((nh, 2, 768, 128), bf16),
            pltpu.VMEM((nh, 2, 256, 128), bf16),
            pltpu.VMEM((6, 5, heads, 128), f32),
            pltpu.VMEM((nh, 256, 768), f32),
            pltpu.VMEM((nh, 256, 768), f32),
            pltpu.VMEM((256, 768), bf16),
            pltpu.VMEM((256, 768), bf16),
            pltpu.VMEM((3, nh, 2, 128), f32),
            pltpu.VMEM((3, nh, 4, 128), f32),
            pltpu.VMEM((2, nh, 4, 128), f32),
            pltpu.VMEM((nh, 4, 128), f32),
            pltpu.VMEM((2, nh, 4, 128), f32),
            pltpu.VMEM((heads, 128, 128), f32),
            pltpu.VMEM((nh, 128, 128), f32),
            pltpu.VMEM((2, nh, 2, 128, 128), bf16),
            pltpu.VMEM((2, heads, 128, 128), bf16),
            pltpu.VMEM((2, nh, 256, 128), bf16),
            dma((nh, 3)),
            dma((nh,)),
            dma((2, nh)),
            dma((2, nh)),
            dma((2, heads)),
            dma((nh,)),
            dma((2, 2)),
            dma((4,)),
            dma((2,)),
            dma((2,)),
            dma((2,)),
            dma,
            dma((2,)),
            dma((2,)),
            dma,
            pltpu.SemaphoreType.REGULAR,
        ],
        compiler_params=pltpu.CompilerParams(
            collective_id=0, has_side_effects=True, vmem_limit_bytes=48000 * 1024
        ),
        name="block_attention",
    )(*args, mask)
    result = pl.pallas_call(
        store,
        out_shape=(out, out, out),
        in_specs=[vmem_spec] * 3,
        out_specs=(hbm_spec,) * 3,
        scratch_shapes=[dma((3,))],
        compiler_params=pltpu.CompilerParams(vmem_limit_bytes=4 * 1024 * 1024),
        name="store_gradients",
    )(*result)
    return tuple(jnp.transpose(x, (1, 0, 2)) for x in result)


def solution(mesh):
    spec = P(("dp", "seq"), None, None)
    return jax.shard_map(
        functools.partial(per_device, seq_size=mesh.shape["seq"]),
        mesh=mesh,
        in_specs=(spec, spec, spec, spec, P()),
        out_specs=(spec, spec, spec),
        check_vma=False,
    )
```
